256 devices in a mesh: replica: 32 (over x, z), shard: 8 (over y, core).
Axes of the slice: x: 4, y: 4, z: 8, core: 2. Of those that a mesh axis runs over, the one named last changes fastest.
Arguments:
- gradient_table: bfloat16 [32, 4096, 768], P('replica', 'shard'), may hold values from -6 to 6
- error_table: float32 [32, 4096, 768], P('replica', 'shard'), may hold values from -6 to 6
- moment_table: float32 [4096, 768], P('shard'), may hold values from -2 to 2
- weight_table: float32 [4096, 768], P('shard'), may hold values from -3 to 3
- start_table: float32 [768, 32], replicated, may hold values from -0.21875 to 0.21875
- gram_table: float32 [2, 32, 32], replicated, as said below
- gradient_query: bfloat16 [32, 768, 768], P('replica', 'shard'), may hold values from -6 to 6
- error_query: float32 [32, 768, 768], P('replica', 'shard'), may hold values from -6 to 6
- moment_query: float32 [768, 768], P('shard'), may hold values from -2 to 2
- weight_query: float32 [768, 768], P('shard'), may hold values from -3 to 3
- start_query: float32 [768, 32], replicated, may hold values from -0.21875 to 0.21875
- gram_query: float32 [2, 32, 32], replicated, as said below
- gradient_norms: float32 [32, 3840], P('replica', 'shard'), may hold values from -6 to 6
- moment_norms: float32 [3840], P('shard'), may hold values from -2 to 2
- weight_norms: float32 [3840], P('shard'), may hold values from 0.5 to 1.5
Outputs:
- residual_table: float32 [32, 4096, 768], P('replica', 'shard')
- velocity_table: float32 [4096, 768], P('shard')
- updated_table: float32 [4096, 768], P('shard')
- warm_table: float32 [768, 32], replicated
- residual_query: float32 [32, 768, 768], P('replica', 'shard')
- velocity_query: float32 [768, 768], P('shard')
- updated_query: float32 [768, 768], P('shard')
- warm_query: float32 [768, 32], replicated
- velocity_norms: float32 [3840], P('shard')
- updated_norms: float32 [3840], P('shard')
The draws below stay inside these ranges and needn't reach their ends.
Inputs may be any that keep to these rules, and one draw needn't show every extreme that they name: `gram_table`: each of the two 32 x 32 matrices is symmetric. `gram_query`: each of the two 32 x 32 matrices is symmetric.
All inputs are finite; a program needn't handle non-finite values.
Results may differ from the reference program's by a relative error of at most 0.0003.
Values sent between devices are 32-bit elements; how exact they have to be, the bound alone decides.
No kernel may reach another device: no remote copies, remote signals or barrier semaphores. Data moves between devices by JAX's collectives and lax.ppermute only.
A program may use at most 64 MiB of HBM per device.

```python
import math
import jax
import jax.numpy as jnp
from jax import lax

D = 768
VOCAB = 4096
RANK = 32
REPLICAS = 32
VEC = 3840


def gram_factor(key, rows):
    noise = jax.random.normal(key, (2, RANK, RANK), jnp.float32)
    symmetric = (noise + jnp.swapaxes(noise, 1, 2)) * 0.70710678
    base = jnp.eye(RANK, dtype=jnp.float32)[None] + 0.3 / math.sqrt(RANK) * symmetric
    scales = jnp.array([rows ** (-0.5), 0.6 * rows ** (-0.25)], jnp.float32)
    return base * scales[:, None, None]


def draw_gram_table(key, part):
    return gram_factor(jax.random.fold_in(key, 11), VOCAB)


def draw_gram_query(key, part):
    return gram_factor(jax.random.fold_in(key, 23), D)


def shard_levels(stream_key, shape, split, low, top_value):
    def one(position, blocks):
        steps = jax.random.uniform(jax.random.fold_in(jax.random.fold_in(stream_key, 6), position), (blocks,), jnp.float32, low / len(split), top_value / len(split))
        return jnp.repeat(jnp.exp(steps), shape[position] // blocks).reshape((-1,) + (1,) * (len(shape) - position - 1))

    gain = one(*split[0])
    for cut in split[1:]:
        gain = gain * one(*cut)
    return gain


def scatter_about(own_key, dims, scale, reach, split=(), kind=jnp.bfloat16):
    result = scale * jax.random.normal(own_key, dims, jnp.float32)
    if split:
        result = result * shard_levels(own_key, dims, split, -0.22, 0.18)
    return jnp.clip(result, -reach, reach).astype(kind)


def setup_inputs(seed: int = 0) -> dict:
    seeds = jax.random.split(jax.random.key(seed), 16)
    gradient_table = scatter_about(seeds[0], (REPLICAS, VOCAB, D), 1.0, 6.0, ((0, 32), (1, 8)))
    error_table = scatter_about(seeds[1], (REPLICAS, VOCAB, D), 1.0, 6.0, ((0, 32), (1, 8)), jnp.float32)
    moment_table = scatter_about(seeds[2], (VOCAB, D), 0.3, 2.0, ((0, 8),), jnp.float32)
    weight_table = scatter_about(seeds[3], (VOCAB, D), 0.5, 3.0, ((0, 8),), jnp.float32)
    start_table = scatter_about(seeds[4], (D, RANK), D ** -0.5, 0.21875, (), jnp.float32)
    gram_table = draw_gram_table(jax.random.fold_in(seeds[15], 71), 0)
    gradient_query = scatter_about(seeds[6], (REPLICAS, D, D), 1.0, 6.0, ((0, 32), (1, 8)))
    error_query = scatter_about(seeds[7], (REPLICAS, D, D), 1.0, 6.0, ((0, 32), (1, 8)), jnp.float32)
    moment_query = scatter_about(seeds[8], (D, D), 0.3, 2.0, ((0, 8),), jnp.float32)
    weight_query = scatter_about(seeds[9], (D, D), 0.5, 3.0, ((0, 8),), jnp.float32)
    start_query = scatter_about(seeds[10], (D, RANK), D ** -0.5, 0.21875, (), jnp.float32)
    gram_query = draw_gram_query(jax.random.fold_in(seeds[15], 71), 0)
    gradient_norms = scatter_about(seeds[12], (REPLICAS, VEC), 1.0, 6.0, ((0, 32), (1, 8)), jnp.float32)
    moment_norms = scatter_about(seeds[13], (VEC,), 0.3, 2.0, ((0, 8),), jnp.float32)
    weight_norms = jnp.clip(1.0 + 0.1 * jax.random.normal(seeds[14], (VEC,), jnp.float32), 0.5, 1.5)
    return dict(gradient_table=gradient_table, error_table=error_table, moment_table=moment_table, weight_table=weight_table, start_table=start_table, gram_table=gram_table, gradient_query=gradient_query, error_query=error_query, moment_query=moment_query, weight_query=weight_query, start_query=start_query, gram_query=gram_query, gradient_norms=gradient_norms, moment_norms=moment_norms, weight_norms=weight_norms)


decay_rate = 0.9
step_rate = 0.01


def compress(gradient, error, start, gram):
    highest = lax.Precision.HIGHEST
    merged = gradient.astype(jnp.float32) + error
    left = jnp.einsum("rmn,nk->mk", merged, start, precision=highest) / REPLICAS
    basis = jnp.dot(left, gram[0], precision=highest, preferred_element_type=jnp.float32)
    right = jnp.einsum("rmn,mk->nk", merged, basis, precision=highest) / REPLICAS
    left = jnp.einsum("rmn,nk->mk", merged, right, precision=highest) / REPLICAS
    basis = jnp.dot(left, gram[1], precision=highest, preferred_element_type=jnp.float32)
    right = jnp.einsum("rmn,mk->nk", merged, basis, precision=highest) / REPLICAS
    approx = jnp.dot(basis, right.T, precision=highest, preferred_element_type=jnp.float32)
    return merged - approx[None], approx, right


def reference(gradient_table, error_table, moment_table, weight_table, start_table, gram_table, gradient_query, error_query, moment_query, weight_query, start_query, gram_query, gradient_norms, moment_norms, weight_norms):
    residual_table, approx_table, warm_table = compress(gradient_table, error_table, start_table, gram_table)
    velocity_table = decay_rate * moment_table + approx_table
    updated_table = weight_table - step_rate * velocity_table
    residual_query, approx_query, warm_query = compress(gradient_query, error_query, start_query, gram_query)
    velocity_query = decay_rate * moment_query + approx_query
    updated_query = weight_query - step_rate * velocity_query
    mean_norms = jnp.sum(gradient_norms, axis=0) / REPLICAS
    velocity_norms = decay_rate * moment_norms + mean_norms
    updated_norms = weight_norms - step_rate * velocity_norms
    return (residual_table, velocity_table, updated_table, warm_table, residual_query, velocity_query, updated_query, warm_query, velocity_norms, updated_norms)
```

```python
import jax
import jax.numpy as jnp
from jax import lax
from jax.sharding import PartitionSpec as P

decay_rate = 0.9
step_rate = 0.01
LANES = 128


def dot(left, right, contract):
    return lax.dot_general(
        left,
        right,
        ((contract[0], contract[1]), ((), ())),
        precision=lax.Precision.HIGHEST,
        preferred_element_type=jnp.float32,
    )


def exchange(blocks, axis):
    return lax.all_to_all(blocks, axis, 0, 0)


def spread(block, axis):
    return exchange(jnp.broadcast_to(block[None], (lax.axis_size(axis),) + block.shape), axis)


def local(
    gradient_table,
    error_table,
    moment_table,
    weight_table,
    start_table,
    gram_table,
    gradient_query,
    error_query,
    moment_query,
    weight_query,
    start_query,
    gram_query,
    gradient_norms,
    moment_norms,
    weight_norms,
):
    replicas = lax.axis_size("replica")
    shards = lax.axis_size("shard")
    rows_table, width = moment_table.shape
    rows_query = moment_query.shape[0]
    rank = start_table.shape[1]
    cols = width // LANES
    per_table = rows_table // replicas
    per_query = rows_query // replicas
    entries = moment_norms.shape[0]
    per_norms = entries // replicas

    merged_table = gradient_table[0].astype(jnp.float32) + error_table[0]
    merged_query = gradient_query[0].astype(jnp.float32) + error_query[0]

    def pack(merged, per):
        blocks = merged.reshape(replicas, per, cols, LANES)
        return blocks.transpose(0, 2, 1, 3).reshape(replicas, per * cols, LANES)

    n_table = per_table * cols
    n_query = per_query * cols
    filled = n_table + n_query
    height = -(-(filled + 1) // 8) * 8
    norms = gradient_norms[0].reshape(replicas, 1, per_norms)
    norms = jnp.pad(norms, ((0, 0), (0, height - filled - 1), (0, LANES - per_norms)))
    sent = jnp.concatenate([pack(merged_table, per_table), pack(merged_query, per_query), norms], axis=1)
    own = jnp.sum(exchange(sent, "replica"), axis=0)

    rows = spread(own, "shard")

    def unpack(part, per):
        blocks = part.reshape(shards, cols, per, LANES).transpose(0, 2, 1, 3)
        return blocks.reshape(shards * per, width)

    sum_table = unpack(rows[:, :n_table], per_table)
    sum_query = unpack(rows[:, n_table:filled], per_query)

    tall = 16
    stack = 2 * rank // tall
    used = cols * stack

    def reduce_right(basis_table, basis_query):
        right = jnp.concatenate(
            [dot(basis_table, sum_table, ((0,), (0,))), dot(basis_query, sum_query, ((0,), (0,)))], axis=0
        )
        blocks = right.reshape(stack, tall, cols, LANES).transpose(2, 0, 1, 3).reshape(used, tall, LANES)
        blocks = jnp.pad(blocks, ((0, replicas - used), (0, 0), (0, 0)))
        return jnp.sum(exchange(blocks, "replica"), axis=0) / replicas

    def stacked(blocks):
        blocks = blocks[:used].reshape(cols, stack, tall, LANES).transpose(1, 2, 0, 3)
        return blocks.reshape(2 * rank, width)

    basis_table = dot(dot(sum_table, start_table, ((1,), (0,))) / replicas, gram_table[0], ((1,), (0,)))
    basis_query = dot(dot(sum_query, start_query, ((1,), (0,))) / replicas, gram_query[0], ((1,), (0,)))
    right = stacked(spread(reduce_right(basis_table, basis_query), "replica"))
    basis_table = dot(dot(sum_table, right[:rank], ((1,), (1,))) / replicas, gram_table[1], ((1,), (0,)))
    basis_query = dot(dot(sum_query, right[rank:], ((1,), (1,))) / replicas, gram_query[1], ((1,), (0,)))

    shard = lax.axis_index("shard")
    high_table = per_table * rank // LANES
    mine_table = lax.dynamic_slice_in_dim(basis_table, shard * per_table, per_table, 0).reshape(high_table, LANES)
    mine_query = lax.dynamic_slice_in_dim(basis_query, shard * per_query, per_query, 0).reshape(1, per_query * rank)
    mine_query = jnp.pad(mine_query, ((0, 0), (0, LANES - per_query * rank)))
    mine_norms = own[filled : filled + 1]
    mine = jnp.concatenate([reduce_right(basis_table, basis_query), mine_table, mine_query, mine_norms], axis=0)
    mine = jnp.pad(mine, ((0, -mine.shape[0] % 8), (0, 0)))
    final = spread(mine, "replica")

    warm = stacked(final[:, :tall])
    basis_table = final[:, tall : tall + high_table].reshape(rows_table, rank)
    basis_query = final[:, tall + high_table, : per_query * rank].reshape(rows_query, rank)
    mean_norms = final[:, tall + high_table + 1, :per_norms].reshape(entries) / replicas

    velocity_norms = decay_rate * moment_norms + mean_norms
    updated_norms = weight_norms - step_rate * velocity_norms
    approx_table = dot(basis_table, warm[:rank], ((1,), (0,)))
    approx_query = dot(basis_query, warm[rank:], ((1,), (0,)))
    velocity_table = decay_rate * moment_table + approx_table
    velocity_query = decay_rate * moment_query + approx_query
    return (
        (merged_table - approx_table)[None],
        velocity_table,
        weight_table - step_rate * velocity_table,
        warm[:rank].T,
        (merged_query - approx_query)[None],
        velocity_query,
        weight_query - step_rate * velocity_query,
        warm[rank:].T,
        velocity_norms,
        updated_norms,
    )


def solution(mesh):
    per_replica = P("replica", "shard", None)
    per_shard = P("shard", None)
    matrix = (per_replica, per_replica, per_shard, per_shard, P(), P())
    return jax.shard_map(
        local,
        mesh=mesh,
        in_specs=matrix + matrix + (P("replica", "shard"), P("shard"), P("shard")),
        out_specs=(per_replica, per_shard, per_shard, P()) * 2 + (P("shard"), P("shard")),
        check_vma=False,
    )
```

```python
import functools

import jax
import jax.numpy as jnp
from jax import lax
from jax.experimental import pallas as pl
from jax.experimental.pallas import tpu as pltpu
from jax.sharding import PartitionSpec as P

decay_rate = 0.9
step_rate = 0.01
LANES = 128
ROWS = 8
VMEM_LIMIT = 24 * 1024 * 1024


def dot(left, right, contract):
    return lax.dot_general(
        left,
        right,
        ((contract[0], contract[1]), ((), ())),
        precision=lax.Precision.HIGHEST,
        preferred_element_type=jnp.float32,
    )


def exchange(blocks, axis, groups=None):
    return lax.all_to_all(blocks, axis, 0, 0, axis_index_groups=groups)


def spread(block, axis):
    return exchange(jnp.broadcast_to(block[None], (lax.axis_size(axis),) + block.shape), axis)


def pack_kernel(gradient, error, rest, merged, sent):
    total = gradient[...].astype(jnp.float32) + error[...]
    merged[...] = total
    blocks = sent.shape[0]
    per = total.shape[0] // blocks
    cols = total.shape[1] // LANES
    for col in range(cols):
        piece = total[:, col * LANES : (col + 1) * LANES].reshape(blocks, per, LANES)
        sent[:, col * per : (col + 1) * per, :] = piece
    sent[:, cols * per :, :] = rest[...]


def pack(gradient, error, rest, steps):
    rows, width = gradient.shape
    blocks = rest.shape[0]
    height = rows // blocks * (width // LANES) + rest.shape[1]
    return pl.pallas_call(
        pack_kernel,
        grid=(steps,),
        in_specs=[
            pl.BlockSpec((rows // steps, width), lambda i: (i, 0)),
            pl.BlockSpec((rows // steps, width), lambda i: (i, 0)),
            pl.BlockSpec((blocks // steps, rest.shape[1], LANES), lambda i: (i, 0, 0)),
        ],
        out_specs=[
            pl.BlockSpec((rows // steps, width), lambda i: (i, 0)),
            pl.BlockSpec((blocks // steps, height, LANES), lambda i: (i, 0, 0)),
        ],
        out_shape=[
            jax.ShapeDtypeStruct((rows, width), jnp.float32),
            jax.ShapeDtypeStruct((blocks, height, LANES), jnp.float32),
        ],
        compiler_params=pltpu.CompilerParams(vmem_limit_bytes=VMEM_LIMIT),
        name="pack",
    )(gradient, error, rest)


def apply(approx, merged, moment, weight, residual, velocity, updated):
    residual[...] = merged - approx
    speed = decay_rate * moment + approx
    velocity[...] = speed
    updated[...] = weight - step_rate * speed


def finish_kernel(
    rank, tiles, every, warm, mt, vt, wt, gq, eq, vq, wq, rt_out, vt_out, ut_out, rq_out, vq_out, uq_out
):
    some = tiles.shape[0]
    tile = tiles[...].reshape(some * ROWS, LANES)
    width = warm.shape[1]
    halves = [
        dot(tile[:, h * rank : (h + 1) * rank], warm[:rank, :], ((1,), (0,))).reshape(some, 1, ROWS, width)
        for h in range(2)
    ]
    approx = jnp.concatenate(halves, axis=1).reshape(2 * some * ROWS, width)
    apply(approx, mt[...], vt[...], wt[...], rt_out, vt_out, ut_out)

    @pl.when(pl.program_id(0) == 0)
    def _():
        per = every.shape[0]
        for i in range(gq.shape[0] // per):
            part = pl.ds(i * per, per)
            basis = every[:, i, :][:, 2 * rank : 3 * rank]
            merged = gq[part, :].astype(jnp.float32) + eq[part, :]
            apply(
                dot(basis, warm[rank:, :], ((1,), (0,))),
                merged,
                vq[part, :],
                wq[part, :],
                rq_out.at[part, :],
                vq_out.at[part, :],
                uq_out.at[part, :],
            )


def finish(rank, steps, tiles, warm, mt, vt, wt, gq, eq, vq, wq):
    rows, width = mt.shape
    rows_query = vq.shape[0]
    moving = pl.BlockSpec((rows // steps, width), lambda i: (i, 0))
    fixed = pl.BlockSpec((rows_query, width), lambda i: (0, 0))
    return pl.pallas_call(
        functools.partial(finish_kernel, rank),
        grid=(steps,),
        in_specs=[
            pl.BlockSpec((tiles.shape[0] // steps, ROWS, LANES), lambda i: (i, 0, 0)),
            pl.BlockSpec(tiles.shape, lambda i: (0, 0, 0)),
            pl.BlockSpec(warm.shape, lambda i: (0, 0)),
            moving,
            moving,
            moving,
            fixed,
            fixed,
            fixed,
            fixed,
        ],
        out_specs=[moving] * 3 + [fixed] * 3,
        out_shape=[jax.ShapeDtypeStruct((rows, width), jnp.float32)] * 3
        + [jax.ShapeDtypeStruct((rows_query, width), jnp.float32)] * 3,
        compiler_params=pltpu.CompilerParams(vmem_limit_bytes=VMEM_LIMIT),
        name="finish",
    )(tiles, tiles, warm, mt, vt, wt, gq, eq, vq, wq)


def local(
    gradient_table,
    error_table,
    moment_table,
    weight_table,
    start_table,
    gram_table,
    gradient_query,
    error_query,
    moment_query,
    weight_query,
    start_query,
    gram_query,
    gradient_norms,
    moment_norms,
    weight_norms,
):
    replicas = lax.axis_size("replica")
    shards = lax.axis_size("shard")
    rows_table, width = moment_table.shape
    rows_query = moment_query.shape[0]
    rank = start_table.shape[1]
    cols = width // LANES
    per_table = rows_table // replicas
    per_query = rows_query // replicas
    entries = moment_norms.shape[0]
    per_norms = entries // replicas
    fours, eights = 4, replicas // 4
    across = [[eights * first + second for first in range(fours)] for second in range(eights)]
    along = [[eights * first + second for second in range(eights)] for first in range(fours)]

    n_table = per_table * cols
    n_query = per_query * cols
    filled = n_table + n_query
    height = -(-(filled + 1) // ROWS) * ROWS
    merged_query = gradient_query[0].astype(jnp.float32) + error_query[0]
    rest = merged_query.reshape(per_query, replicas, cols, LANES).transpose(1, 0, 2, 3)
    norms = gradient_norms[0].reshape(replicas, 1, per_norms)
    norms = jnp.pad(norms, ((0, 0), (0, height - filled - 1), (0, LANES - per_norms)))
    rest = jnp.concatenate([rest.reshape(replicas, n_query, LANES), norms], axis=1)
    merged_table, sent = pack(gradient_table[0], error_table[0], rest, fours)

    blocks = sent.reshape(fours, eights * height, LANES)
    blocks = jnp.sum(exchange(blocks, "replica", across), axis=0).reshape(eights, height, LANES)
    own = jnp.sum(exchange(blocks, "replica", along), axis=0)

    rows = spread(own, "shard")

    sum_table = rows[:, :n_table].reshape(shards, cols, per_table, LANES).transpose(0, 2, 1, 3)
    sum_table = sum_table.reshape(shards * per_table, width)
    sum_query = rows[:, n_table:filled].reshape(shards * per_query, width)

    tall = 16
    stack = 2 * rank // tall
    used = cols * stack

    def reduce_right(basis_table, basis_query):
        right = jnp.concatenate(
            [dot(basis_table, sum_table, ((0,), (0,))), dot(basis_query, sum_query, ((0,), (0,)))], axis=0
        )
        blocks = right.reshape(stack, tall, cols, LANES).transpose(2, 0, 1, 3).reshape(used, tall, LANES)
        blocks = jnp.pad(blocks, ((0, replicas - used), (0, 0), (0, 0)))
        return jnp.sum(exchange(blocks, "replica"), axis=0) / replicas

    def stacked(blocks):
        blocks = blocks[:used].reshape(cols, stack, tall, LANES).transpose(1, 2, 0, 3)
        return blocks.reshape(2 * rank, width)

    basis_table = dot(dot(sum_table, start_table, ((1,), (0,))) / replicas, gram_table[0], ((1,), (0,)))
    basis_query = dot(dot(sum_query, start_query, ((1,), (0,))) / replicas, gram_query[0], ((1,), (0,)))
    right = stacked(spread(reduce_right(basis_table, basis_query), "replica"))
    basis_table = dot(dot(sum_table, right[:rank], ((1,), (1,))) / replicas, gram_table[1], ((1,), (0,)))
    basis_query = dot(dot(sum_query, right[rank:], ((1,), (1,))) / replicas, gram_query[1], ((1,), (0,)))

    shard = lax.axis_index("shard")
    mine_table = lax.dynamic_slice_in_dim(basis_table, shard * per_table, per_table, 0)
    mine_query = lax.dynamic_slice_in_dim(basis_query, shard * per_query, per_query, 0)
    mine_query = jnp.pad(mine_query, ((0, ROWS - per_query), (0, 0)))
    mine_norms = jnp.pad(own[filled : filled + 1, :rank], ((0, ROWS - 1), (0, 0)))
    mine = jnp.concatenate([mine_table[:ROWS], mine_table[ROWS:], mine_query, mine_norms], axis=1)
    mine = jnp.concatenate([mine, reduce_right(basis_table, basis_query)], axis=0)
    final = spread(mine, "replica")

    tiles = final[:, :ROWS]
    warm = stacked(final[:, ROWS:])
    mean_norms = final[:, 0, 3 * rank : 3 * rank + per_norms].reshape(entries) / replicas
    velocity_norms = decay_rate * moment_norms + mean_norms
    updated_norms = weight_norms - step_rate * velocity_norms
    residual_table, velocity_table, updated_table, residual_query, velocity_query, updated_query = finish(
        rank,
        4,
        tiles,
        warm,
        merged_table,
        moment_table,
        weight_table,
        gradient_query[0],
        error_query[0],
        moment_query,
        weight_query,
    )
    return (
        residual_table[None],
        velocity_table,
        updated_table,
        warm[:rank].T,
        residual_query[None],
        velocity_query,
        updated_query,
        warm[rank:].T,
        velocity_norms,
        updated_norms,
    )


def solution(mesh):
    per_replica = P("replica", "shard", None)
    per_shard = P("shard", None)
    matrix = (per_replica, per_replica, per_shard, per_shard, P(), P())
    return jax.shard_map(
        local,
        mesh=mesh,
        in_specs=matrix + matrix + (P("replica", "shard"), P("shard"), P("shard")),
        out_specs=(per_replica, per_shard, per_shard, P()) * 2 + (P("shard"), P("shard")),
        check_vma=False,
    )
```

```python
import functools

import jax
import jax.numpy as jnp
from jax import lax
from jax.experimental import pallas as pl
from jax.experimental.pallas import tpu as pltpu
from jax.sharding import PartitionSpec as P

decay_rate = 0.9
step_rate = 0.01
LANES = 128
ROWS = 8
VMEM_LIMIT = 24 * 1024 * 1024


def dot(left, right, contract):
    return lax.dot_general(
        left,
        right,
        ((contract[0], contract[1]), ((), ())),
        precision=lax.Precision.HIGHEST,
        preferred_element_type=jnp.float32,
    )


def exchange(blocks, axis, groups=None):
    return lax.all_to_all(blocks, axis, 0, 0, axis_index_groups=groups)


def spread(block, axis):
    return exchange(jnp.broadcast_to(block[None], (lax.axis_size(axis),) + block.shape), axis)


def pack_kernel(gradient, error, rest, sent):
    total = gradient[...].astype(jnp.float32) + error[...]
    blocks = sent.shape[0]
    per = total.shape[0] // blocks
    cols = total.shape[1] // LANES
    for col in range(cols):
        piece = total[:, col * LANES : (col + 1) * LANES].reshape(blocks, per, LANES)
        sent[:, col * per : (col + 1) * per, :] = piece
    sent[:, cols * per :, :] = rest[...]


def pack(gradient, error, rest, steps):
    rows, width = gradient.shape
    blocks = rest.shape[0]
    height = rows // blocks * (width // LANES) + rest.shape[1]
    return pl.pallas_call(
        pack_kernel,
        grid=(steps,),
        in_specs=[
            pl.BlockSpec((rows // steps, width), lambda i: (i, 0)),
            pl.BlockSpec((rows // steps, width), lambda i: (i, 0)),
            pl.BlockSpec((blocks // steps, rest.shape[1], LANES), lambda i: (i, 0, 0)),
        ],
        out_specs=pl.BlockSpec((blocks // steps, height, LANES), lambda i: (i, 0, 0)),
        out_shape=jax.ShapeDtypeStruct((blocks, height, LANES), jnp.float32),
        compiler_params=pltpu.CompilerParams(vmem_limit_bytes=VMEM_LIMIT),
        name="pack",
    )(gradient, error, rest)


def apply(approx, merged, moment, weight, residual, velocity, updated):
    residual[...] = merged - approx
    speed = decay_rate * moment + approx
    velocity[...] = speed
    updated[...] = weight - step_rate * speed


def finish_kernel(
    rank, core, mine, other, gt, et, vt, wt, gq, eq, vq, wq,
    rt_out, vt_out, ut_out, warm_table, rq_out, vq_out, uq_out, warm_query, tiles,
):
    step = pl.program_id(0)
    replicas = mine.shape[0]
    width = gt.shape[1]
    cols = width // LANES
    stack = rank // ROWS

    def pick(first, second):
        return jnp.where(core[0] == 0, first, second)

    def own(part):
        flat = part.reshape(replicas * ROWS, LANES)
        return pick(flat, pltpu.roll(flat, LANES // 2, 1)).reshape(replicas, ROWS, LANES)

    @pl.when(step == 0)
    def _():
        here, there = mine[...], other[...]
        for out, block in ((warm_table, pick(here, there)), (warm_query, pick(there, here))):
            for col in range(cols):
                for row in range(stack):
                    piece = block[col * stack + row, ROWS:, :]
                    out[row * ROWS : (row + 1) * ROWS, col * LANES : (col + 1) * LANES] = piece
        tiles[0] = own(pick(here[:, :ROWS, :], there[:, :ROWS, :]))
        tiles[1] = own(pick(there[:, :ROWS, :], here[:, :ROWS, :]))
        for i in range(gq.shape[0] // replicas):
            part = pl.ds(i * replicas, replicas)
            basis = tiles[1, :, i, :][:, :rank]
            merged = gq[part, :].astype(jnp.float32) + eq[part, :]
            apply(
                dot(basis, warm_query[...], ((1,), (0,))),
                merged,
                vq[part, :],
                wq[part, :],
                rq_out.at[part, :],
                vq_out.at[part, :],
                uq_out.at[part, :],
            )

    some = gt.shape[0] // (2 * ROWS)
    tile = tiles[0, pl.ds(pl.multiple_of(step * some, some), some)].reshape(some * ROWS, LANES)
    halves = [
        dot(tile[:, h * rank : (h + 1) * rank], warm_table[...], ((1,), (0,))).reshape(some, 1, ROWS, width)
        for h in range(2)
    ]
    approx = jnp.concatenate(halves, axis=1).reshape(2 * some * ROWS, width)
    merged = gt[...].astype(jnp.float32) + et[...]
    apply(approx, merged, vt[...], wt[...], rt_out, vt_out, ut_out)


def finish(rank, steps, core, mine, other, gt, et, vt, wt, gq, eq, vq, wq):
    rows, width = gt.shape
    rows_query = gq.shape[0]
    moving = pl.BlockSpec((rows // steps, width), lambda i: (i, 0))
    fixed = pl.BlockSpec((rows_query, width), lambda i: (0, 0))
    factor = pl.BlockSpec((rank, width), lambda i: (0, 0))
    whole = pl.BlockSpec(mine.shape, lambda i: (0, 0, 0))
    shape = functools.partial(jax.ShapeDtypeStruct, dtype=jnp.float32)
    return pl.pallas_call(
        functools.partial(finish_kernel, rank),
        grid=(steps,),
        in_specs=[pl.BlockSpec(memory_space=pltpu.SMEM), whole, whole] + [moving] * 4 + [fixed] * 4,
        out_specs=[moving] * 3 + [factor] + [fixed] * 3 + [factor],
        out_shape=[shape((rows, width))] * 3
        + [shape((rank, width))]
        + [shape((rows_query, width))] * 3
        + [shape((rank, width))],
        scratch_shapes=[pltpu.VMEM((2, mine.shape[0], ROWS, LANES), jnp.float32)],
        compiler_params=pltpu.CompilerParams(vmem_limit_bytes=VMEM_LIMIT),
        name="finish",
    )(core, mine, other, gt, et, vt, wt, gq, eq, vq, wq)


def local(
    gradient_table,
    error_table,
    moment_table,
    weight_table,
    start_table,
    gram_table,
    gradient_query,
    error_query,
    moment_query,
    weight_query,
    start_query,
    gram_query,
    gradient_norms,
    moment_norms,
    weight_norms,
):
    replicas = lax.axis_size("replica")
    shards = lax.axis_size("shard")
    rows_table, width = moment_table.shape
    rows_query = moment_query.shape[0]
    rank = start_table.shape[1]
    cols = width // LANES
    per_table = rows_table // replicas
    per_query = rows_query // replicas
    entries = moment_norms.shape[0]
    fours, eights = 4, replicas // 4
    across = [[eights * first + second for first in range(fours)] for second in range(eights)]
    along = [[eights * first + second for second in range(eights)] for first in range(fours)]

    n_table = per_table * cols
    n_query = per_query * cols
    n_norms = -(-entries // LANES)
    filled = n_table + n_query
    height = -(-(filled + n_norms) // ROWS) * ROWS
    merged_query = gradient_query[0].astype(jnp.float32) + error_query[0]
    rest = merged_query.reshape(per_query, replicas, cols, LANES).transpose(1, 0, 2, 3)
    norms = jnp.pad(gradient_norms, ((0, 0), (0, n_norms * LANES - entries))).reshape(1, n_norms, LANES)
    norms = jnp.broadcast_to(norms, (replicas, n_norms, LANES))
    rest = jnp.concatenate([rest.reshape(replicas, n_query, LANES), norms], axis=1)
    rest = jnp.pad(rest, ((0, 0), (0, height - filled - n_norms), (0, 0)))
    sent = pack(gradient_table[0], error_table[0], rest, fours)

    blocks = sent.reshape(fours, eights * height, LANES)
    blocks = jnp.sum(exchange(blocks, "replica", across), axis=0).reshape(eights, height, LANES)
    own = jnp.sum(exchange(blocks, "replica", along), axis=0)

    mean_norms = own[filled : filled + n_norms].reshape(n_norms * LANES)[:entries] / replicas
    velocity_norms = decay_rate * moment_norms + mean_norms
    updated_norms = weight_norms - step_rate * velocity_norms

    shard = lax.axis_index("shard")
    core = shard % 2
    query = own[n_table:filled].reshape(per_query, cols, LANES).transpose(1, 0, 2)
    query = jnp.pad(query, ((0, 0), (0, per_table - per_query), (0, 0))).reshape(n_table, LANES)
    both = jnp.stack([own[:n_table], query])
    both = jnp.broadcast_to(both[None], (shards // 2, 2, n_table, LANES)).reshape(shards, n_table, LANES)
    total = exchange(both, "shard").reshape(shards, cols, per_table, LANES).transpose(0, 2, 1, 3)
    total = total.reshape(shards * per_table, width)
    start = jnp.where(core == 0, start_table, start_query)
    gram = jnp.where(core == 0, gram_table, gram_query)

    stack = rank // ROWS
    used = cols * stack

    def reduce_right(basis):
        blocks = dot(basis, total, ((0,), (0,))).reshape(stack, ROWS, cols, LANES)
        blocks = blocks.transpose(2, 0, 1, 3).reshape(used, ROWS, LANES)
        blocks = jnp.pad(blocks, ((0, replicas - used), (0, 0), (0, 0)))
        return jnp.sum(exchange(blocks, "replica"), axis=0) / replicas

    basis = dot(dot(total, start, ((1,), (0,))) / replicas, gram[0], ((1,), (0,)))
    right = spread(reduce_right(basis), "replica")[:used]
    right = right.reshape(cols, stack, ROWS, LANES).transpose(1, 2, 0, 3).reshape(rank, width)
    basis = dot(dot(total, right, ((1,), (1,))) / replicas, gram[1], ((1,), (0,)))

    chip = lax.dynamic_slice_in_dim(basis, shard // 2 * (2 * per_table), 2 * per_table, 0)
    chip = jnp.concatenate([chip[i * ROWS : (i + 1) * ROWS] for i in range(2 * per_table // ROWS)], axis=1)
    mine = spread(jnp.concatenate([chip, reduce_right(basis)], axis=0), "replica")
    other = lax.ppermute(mine, "shard", [(i, i ^ 1) for i in range(shards)])
    (
        residual_table,
        velocity_table,
        updated_table,
        warm_table,
        residual_query,
        velocity_query,
        updated_query,
        warm_query,
    ) = finish(
        rank,
        4,
        core.reshape(1),
        mine,
        other,
        gradient_table[0],
        error_table[0],
        moment_table,
        weight_table,
        gradient_query[0],
        error_query[0],
        moment_query,
        weight_query,
    )
    return (
        residual_table[None],
        velocity_table,
        updated_table,
        warm_table.T,
        residual_query[None],
        velocity_query,
        updated_query,
        warm_query.T,
        velocity_norms,
        updated_norms,
    )


def solution(mesh):
    per_replica = P("replica", "shard", None)
    per_shard = P("shard", None)
    matrix = (per_replica, per_replica, per_shard, per_shard, P(), P())
    return jax.shard_map(
        local,
        mesh=mesh,
        in_specs=matrix + matrix + (P("replica", "shard"), P("shard"), P("shard")),
        out_specs=(per_replica, per_shard, per_shard, P()) * 2 + (P("shard"), P("shard")),
        check_vma=False,
    )
```

```python
import functools

import jax
import jax.numpy as jnp
from jax import lax
from jax.experimental import pallas as pl
from jax.experimental.pallas import tpu as pltpu
from jax.sharding import PartitionSpec as P

decay_rate = 0.9
step_rate = 0.01
LANES = 128
ROWS = 8
VMEM_LIMIT = 24 * 1024 * 1024
VMEM_ALL = 63 * 1024 * 1024


def dot(left, right, contract):
    return lax.dot_general(
        left,
        right,
        ((contract[0], contract[1]), ((), ())),
        precision=lax.Precision.HIGHEST,
        preferred_element_type=jnp.float32,
    )


def exchange(blocks, axis, groups=None):
    return lax.all_to_all(blocks, axis, 0, 0, axis_index_groups=groups)


def spread(block, axis):
    return exchange(jnp.broadcast_to(block[None], (lax.axis_size(axis),) + block.shape), axis)


def pack_kernel(gradient, error, rest, sent):
    total = gradient[...].astype(jnp.float32) + error[...]
    blocks = sent.shape[0]
    per = total.shape[0] // blocks
    cols = total.shape[1] // LANES
    for col in range(cols):
        piece = total[:, col * LANES : (col + 1) * LANES].reshape(blocks, per, LANES)
        sent[:, col * per : (col + 1) * per, :] = piece
    sent[:, cols * per :, :] = rest[...]


def pack(gradient, error, rest, steps):
    rows, width = gradient.shape
    blocks = rest.shape[0]
    height = rows // blocks * (width // LANES) + rest.shape[1]
    return pl.pallas_call(
        pack_kernel,
        grid=(steps,),
        in_specs=[
            pl.BlockSpec((rows // steps, width), lambda i: (i, 0)),
            pl.BlockSpec((rows // steps, width), lambda i: (i, 0)),
            pl.BlockSpec((blocks // steps, rest.shape[1], LANES), lambda i: (i, 0, 0)),
        ],
        out_specs=pl.BlockSpec((blocks // steps, height, LANES), lambda i: (i, 0, 0)),
        out_shape=jax.ShapeDtypeStruct((blocks, height, LANES), jnp.float32),
        compiler_params=pltpu.CompilerParams(vmem_limit_bytes=VMEM_LIMIT),
        name="pack",
    )(gradient, error, rest)


def apply(approx, merged, moment, weight, residual, velocity, updated):
    residual[...] = merged - approx
    speed = decay_rate * moment + approx
    velocity[...] = speed
    updated[...] = weight - step_rate * speed


def finish_kernel(
    rank, core, mine, other, gt, et, vt, wt, gq, eq, vq, wq,
    rt_out, vt_out, ut_out, warm_table, rq_out, vq_out, uq_out, warm_query, tiles,
):
    step = pl.program_id(0)
    replicas = mine.shape[0]
    width = gt.shape[1]
    cols = width // LANES
    stack = rank // ROWS

    def pick(first, second):
        return jnp.where(core[0] == 0, first, second)

    def own(part):
        flat = part.reshape(replicas * ROWS, LANES)
        return pick(flat, pltpu.roll(flat, LANES // 2, 1)).reshape(replicas, ROWS, LANES)

    @pl.when(step == 0)
    def _():
        here, there = mine[...], other[...]
        for out, block in ((warm_table, pick(here, there)), (warm_query, pick(there, here))):
            for col in range(cols):
                for row in range(stack):
                    piece = block[col * stack + row, ROWS:, :]
                    out[row * ROWS : (row + 1) * ROWS, col * LANES : (col + 1) * LANES] = piece
        tiles[0] = own(pick(here[:, :ROWS, :], there[:, :ROWS, :]))
        tiles[1] = own(pick(there[:, :ROWS, :], here[:, :ROWS, :]))
        for i in range(gq.shape[0] // replicas):
            part = pl.ds(i * replicas, replicas)
            basis = tiles[1, :, i, :][:, :rank]
            merged = gq[part, :].astype(jnp.float32) + eq[part, :]
            apply(
                dot(basis, warm_query[...], ((1,), (0,))),
                merged,
                vq[part, :],
                wq[part, :],
                rq_out.at[part, :],
                vq_out.at[part, :],
                uq_out.at[part, :],
            )

    some = gt.shape[0] // (2 * ROWS)
    tile = tiles[0, pl.ds(pl.multiple_of(step * some, some), some)].reshape(some * ROWS, LANES)
    halves = [
        dot(tile[:, h * rank : (h + 1) * rank], warm_table[...], ((1,), (0,))).reshape(some, 1, ROWS, width)
        for h in range(2)
    ]
    approx = jnp.concatenate(halves, axis=1).reshape(2 * some * ROWS, width)
    merged = gt[...].astype(jnp.float32) + et[...]
    apply(approx, merged, vt[...], wt[...], rt_out, vt_out, ut_out)


def finish(rank, steps, core, mine, other, gt, et, vt, wt, gq, eq, vq, wq):
    rows, width = gt.shape
    rows_query = gq.shape[0]
    moving = pl.BlockSpec((rows // steps, width), lambda i: (i, 0))
    fixed = pl.BlockSpec((rows_query, width), lambda i: (0, 0))
    factor = pl.BlockSpec((rank, width), lambda i: (0, 0))
    whole = pl.BlockSpec(mine.shape, lambda i: (0, 0, 0))
    shape = functools.partial(jax.ShapeDtypeStruct, dtype=jnp.float32)
    return pl.pallas_call(
        functools.partial(finish_kernel, rank),
        grid=(steps,),
        in_specs=[pl.BlockSpec(memory_space=pltpu.SMEM), whole, whole] + [moving] * 4 + [fixed] * 4,
        out_specs=[moving] * 3 + [factor] + [fixed] * 3 + [factor],
        out_shape=[shape((rows, width))] * 3
        + [shape((rank, width))]
        + [shape((rows_query, width))] * 3
        + [shape((rank, width))],
        scratch_shapes=[pltpu.VMEM((2, mine.shape[0], ROWS, LANES), jnp.float32)],
        compiler_params=pltpu.CompilerParams(vmem_limit_bytes=VMEM_ALL),
        name="finish",
    )(core, mine, other, gt, et, vt, wt, gq, eq, vq, wq)


def local(
    gradient_table,
    error_table,
    moment_table,
    weight_table,
    start_table,
    gram_table,
    gradient_query,
    error_query,
    moment_query,
    weight_query,
    start_query,
    gram_query,
    gradient_norms,
    moment_norms,
    weight_norms,
):
    replicas = lax.axis_size("replica")
    shards = lax.axis_size("shard")
    rows_table, width = moment_table.shape
    rows_query = moment_query.shape[0]
    rank = start_table.shape[1]
    cols = width // LANES
    per_table = rows_table // replicas
    per_query = rows_query // replicas
    entries = moment_norms.shape[0]
    fours, eights = 4, replicas // 4
    across = [[eights * first + second for first in range(fours)] for second in range(eights)]
    along = [[eights * first + second for second in range(eights)] for first in range(fours)]

    n_table = per_table * cols
    n_query = per_query * cols
    n_norms = -(-entries // LANES)
    filled = n_table + n_query
    height = -(-(filled + n_norms) // ROWS) * ROWS
    merged_query = gradient_query[0].astype(jnp.float32) + error_query[0]
    rest = merged_query.reshape(per_query, replicas, cols, LANES).transpose(1, 0, 2, 3)
    norms = jnp.pad(gradient_norms, ((0, 0), (0, n_norms * LANES - entries))).reshape(1, n_norms, LANES)
    norms = jnp.broadcast_to(norms, (replicas, n_norms, LANES))
    rest = jnp.concatenate([rest.reshape(replicas, n_query, LANES), norms], axis=1)
    rest = jnp.pad(rest, ((0, 0), (0, height - filled - n_norms), (0, 0)))
    sent = pack(gradient_table[0], error_table[0], rest, fours)

    blocks = sent.reshape(fours, eights * height, LANES)
    blocks = jnp.sum(exchange(blocks, "replica", across), axis=0).reshape(eights, height, LANES)
    own = jnp.sum(exchange(blocks, "replica", along), axis=0)

    mean_norms = own[filled : filled + n_norms].reshape(n_norms * LANES)[:entries] / replicas
    velocity_norms = decay_rate * moment_norms + mean_norms
    updated_norms = weight_norms - step_rate * velocity_norms

    shard = lax.axis_index("shard")
    core = shard % 2
    query = own[n_table:filled].reshape(per_query, cols, LANES).transpose(1, 0, 2)
    query = jnp.pad(query, ((0, 0), (0, per_table - per_query), (0, 0))).reshape(n_table, LANES)
    both = jnp.stack([own[:n_table], query])
    both = jnp.broadcast_to(both[None], (shards // 2, 2, n_table, LANES)).reshape(shards, n_table, LANES)
    start = jnp.where(core == 0, start_table, start_query)
    gram = jnp.where(core == 0, gram_table, gram_query)
    total, start, gram, velocity_norms, updated_norms = lax.optimization_barrier(
        (exchange(both, "shard"), start, gram, velocity_norms, updated_norms)
    )
    total = total.reshape(shards, cols, per_table, LANES).transpose(0, 2, 1, 3)
    total = total.reshape(shards * per_table, width)

    stack = rank // ROWS
    used = cols * stack

    def reduce_right(basis):
        blocks = dot(basis, total, ((0,), (0,))).reshape(stack, ROWS, cols, LANES)
        blocks = blocks.transpose(2, 0, 1, 3).reshape(used, ROWS, LANES)
        blocks = jnp.pad(blocks, ((0, replicas - used), (0, 0), (0, 0)))
        return jnp.sum(exchange(blocks, "replica"), axis=0) / replicas

    basis = dot(dot(total, start, ((1,), (0,))) / replicas, gram[0], ((1,), (0,)))
    right = spread(reduce_right(basis), "replica")[:used]
    right = right.reshape(cols, stack, ROWS, LANES).transpose(1, 2, 0, 3).reshape(rank, width)
    basis = dot(dot(total, right, ((1,), (1,))) / replicas, gram[1], ((1,), (0,)))

    chip = lax.dynamic_slice_in_dim(basis, shard // 2 * (2 * per_table), 2 * per_table, 0)
    chip = jnp.concatenate([chip[i * ROWS : (i + 1) * ROWS] for i in range(2 * per_table // ROWS)], axis=1)
    mine = spread(jnp.concatenate([chip, reduce_right(basis)], axis=0), "replica")
    other = lax.ppermute(mine, "shard", [(i, i ^ 1) for i in range(shards)])
    (
        residual_table,
        velocity_table,
        updated_table,
        warm_table,
        residual_query,
        velocity_query,
        updated_query,
        warm_query,
    ) = finish(
        rank,
        4,
        core.reshape(1),
        mine,
        other,
        gradient_table[0],
        error_table[0],
        moment_table,
        weight_table,
        gradient_query[0],
        error_query[0],
        moment_query,
        weight_query,
    )
    return (
        residual_table[None],
        velocity_table,
        updated_table,
        warm_table.T,
        residual_query[None],
        velocity_query,
        updated_query,
        warm_query.T,
        velocity_norms,
        updated_norms,
    )


def solution(mesh):
    per_replica = P("replica", "shard", None)
    per_shard = P("shard", None)
    matrix = (per_replica, per_replica, per_shard, per_shard, P(), P())
    return jax.shard_map(
        local,
        mesh=mesh,
        in_specs=matrix + matrix + (P("replica", "shard"), P("shard"), P("shard")),
        out_specs=(per_replica, per_shard, per_shard, P()) * 2 + (P("shard"), P("shard")),
        check_vma=False,
    )
```

```python
import functools

import jax
import jax.numpy as jnp
from jax import lax
from jax.experimental import pallas as pl
from jax.experimental.pallas import tpu as pltpu
from jax.sharding import PartitionSpec as P

decay_rate = 0.9
step_rate = 0.01
LANES = 128
ROWS = 8
VMEM_LIMIT = 24 * 1024 * 1024
VMEM_ALL = 63 * 1024 * 1024


def dot(left, right, contract):
    return lax.dot_general(
        left,
        right,
        ((contract[0], contract[1]), ((), ())),
        precision=lax.Precision.HIGHEST,
        preferred_element_type=jnp.float32,
    )


def exchange(blocks, axis, groups=None):
    return lax.all_to_all(blocks, axis, 0, 0, axis_index_groups=groups)


def spread(block, axis):
    return exchange(jnp.broadcast_to(block[None], (lax.axis_size(axis),) + block.shape), axis)


def pack_kernel(first, gradient, error, rest, sent):
    total = gradient[...].astype(jnp.float32) + error[...]
    blocks = sent.shape[0]
    per = total.shape[0] // blocks
    cols = total.shape[1] // LANES
    for col in range(cols):
        piece = total[:, col * LANES : (col + 1) * LANES].reshape(blocks, per, LANES)
        sent[:, col * per : (col + 1) * per, :] = piece
    sent[:, cols * per :, :] = rest[...]


def pack(first, gradient, error, rest, steps):
    rows, width = gradient.shape
    blocks = rest.shape[0]
    height = rows // blocks * (width // LANES) + rest.shape[1]
    def source(i, first):
        return lax.rem(first[0] + i, steps)

    rows_spec = pl.BlockSpec((rows // steps, width), lambda i, first: (source(i, first), 0))
    return pl.pallas_call(
        pack_kernel,
        grid_spec=pltpu.PrefetchScalarGridSpec(
            num_scalar_prefetch=1,
            grid=(steps,),
            in_specs=[
                rows_spec,
                rows_spec,
                pl.BlockSpec((blocks // steps, rest.shape[1], LANES), lambda i, first: (source(i, first), 0, 0)),
            ],
            out_specs=pl.BlockSpec((blocks // steps, height, LANES), lambda i, first: (i, 0, 0)),
        ),
        out_shape=jax.ShapeDtypeStruct((blocks, height, LANES), jnp.float32),
        compiler_params=pltpu.CompilerParams(vmem_limit_bytes=VMEM_LIMIT),
        name="pack",
    )(first, gradient, error, rest)


def apply(approx, merged, moment, weight, residual, velocity, updated):
    residual[...] = merged - approx
    speed = decay_rate * moment + approx
    velocity[...] = speed
    updated[...] = weight - step_rate * speed


def finish_kernel(
    rank, core, mine, other, gt, et, vt, wt, gq, eq, vq, wq,
    rt_out, vt_out, ut_out, warm_table, rq_out, vq_out, uq_out, warm_query, tiles,
):
    step = pl.program_id(0)
    replicas = mine.shape[0]
    width = gt.shape[1]
    cols = width // LANES
    stack = rank // ROWS

    def pick(first, second):
        return jnp.where(core[0] == 0, first, second)

    def own(part):
        flat = part.reshape(replicas * ROWS, LANES)
        return pick(flat, pltpu.roll(flat, LANES // 2, 1)).reshape(replicas, ROWS, LANES)

    @pl.when(step == 0)
    def _():
        here, there = mine[...], other[...]
        for out, block in ((warm_table, pick(here, there)), (warm_query, pick(there, here))):
            for col in range(cols):
                for row in range(stack):
                    piece = block[col * stack + row, ROWS:, :]
                    out[row * ROWS : (row + 1) * ROWS, col * LANES : (col + 1) * LANES] = piece
        tiles[0] = own(pick(here[:, :ROWS, :], there[:, :ROWS, :]))
        tiles[1] = own(pick(there[:, :ROWS, :], here[:, :ROWS, :]))
        for i in range(gq.shape[0] // replicas):
            part = pl.ds(i * replicas, replicas)
            basis = tiles[1, :, i, :][:, :rank]
            merged = gq[part, :].astype(jnp.float32) + eq[part, :]
            apply(
                dot(basis, warm_query[...], ((1,), (0,))),
                merged,
                vq[part, :],
                wq[part, :],
                rq_out.at[part, :],
                vq_out.at[part, :],
                uq_out.at[part, :],
            )

    some = gt.shape[0] // (2 * ROWS)
    tile = tiles[0, pl.ds(pl.multiple_of(step * some, some), some)].reshape(some * ROWS, LANES)
    halves = [
        dot(tile[:, h * rank : (h + 1) * rank], warm_table[...], ((1,), (0,))).reshape(some, 1, ROWS, width)
        for h in range(2)
    ]
    approx = jnp.concatenate(halves, axis=1).reshape(2 * some * ROWS, width)
    merged = gt[...].astype(jnp.float32) + et[...]
    apply(approx, merged, vt[...], wt[...], rt_out, vt_out, ut_out)


def finish(rank, steps, core, mine, other, gt, et, vt, wt, gq, eq, vq, wq):
    rows, width = gt.shape
    rows_query = gq.shape[0]
    moving = pl.BlockSpec((rows // steps, width), lambda i: (i, 0))
    fixed = pl.BlockSpec((rows_query, width), lambda i: (0, 0))
    factor = pl.BlockSpec((rank, width), lambda i: (0, 0))
    whole = pl.BlockSpec(mine.shape, lambda i: (0, 0, 0))
    shape = functools.partial(jax.ShapeDtypeStruct, dtype=jnp.float32)
    return pl.pallas_call(
        functools.partial(finish_kernel, rank),
        grid=(steps,),
        in_specs=[pl.BlockSpec(memory_space=pltpu.SMEM), whole, whole] + [moving] * 4 + [fixed] * 4,
        out_specs=[moving] * 3 + [factor] + [fixed] * 3 + [factor],
        out_shape=[shape((rows, width))] * 3
        + [shape((rank, width))]
        + [shape((rows_query, width))] * 3
        + [shape((rank, width))],
        scratch_shapes=[pltpu.VMEM((2, mine.shape[0], ROWS, LANES), jnp.float32)],
        compiler_params=pltpu.CompilerParams(vmem_limit_bytes=VMEM_ALL),
        name="finish",
    )(core, mine, other, gt, et, vt, wt, gq, eq, vq, wq)


def local(
    gradient_table,
    error_table,
    moment_table,
    weight_table,
    start_table,
    gram_table,
    gradient_query,
    error_query,
    moment_query,
    weight_query,
    start_query,
    gram_query,
    gradient_norms,
    moment_norms,
    weight_norms,
):
    replicas = lax.axis_size("replica")
    shards = lax.axis_size("shard")
    rows_table, width = moment_table.shape
    rows_query = moment_query.shape[0]
    rank = start_table.shape[1]
    cols = width // LANES
    per_table = rows_table // replicas
    per_query = rows_query // replicas
    entries = moment_norms.shape[0]
    fours, eights = 4, replicas // 4
    along = [[eights * first + second for second in range(eights)] for first in range(fours)]

    n_table = per_table * cols
    n_query = per_query * cols
    n_norms = -(-entries // LANES)
    filled = n_table + n_query
    height = -(-(filled + n_norms) // ROWS) * ROWS
    merged_query = gradient_query[0].astype(jnp.float32) + error_query[0]
    rest = merged_query.reshape(per_query, replicas, cols, LANES).transpose(1, 0, 2, 3)
    norms = jnp.pad(gradient_norms, ((0, 0), (0, n_norms * LANES - entries))).reshape(1, n_norms, LANES)
    norms = jnp.broadcast_to(norms, (replicas, n_norms, LANES))
    rest = jnp.concatenate([rest.reshape(replicas, n_query, LANES), norms], axis=1)
    rest = jnp.pad(rest, ((0, 0), (0, height - filled - n_norms), (0, 0)))
    first = lax.axis_index("replica") // eights
    sent = pack(first.reshape(1), gradient_table[0], error_table[0], rest, fours)
    sent = sent.reshape(fours, 2, eights // 2, height, LANES)

    def shift(block, by):
        pairs = [(f * eights + e, (f + by) % fours * eights + e) for f in range(fours) for e in range(eights)]
        return lax.ppermute(block, "replica", pairs)

    ahead = shift(sent[2, 0], 1)
    back = shift(sent[2, 1], fours - 1)
    right_one = shift(sent[1, 1], 1)
    left_zero = shift(sent[3, 0], fours - 1)
    right_zero = shift(sent[1, 0] + ahead, 1)
    left_one = shift(sent[3, 1] + back, fours - 1)
    zero = sent[0, 0] + left_zero + right_zero
    one = sent[0, 1] + right_one + left_one
    blocks = jnp.concatenate([zero, one], axis=0)
    own = jnp.sum(exchange(blocks, "replica", along), axis=0)

    mean_norms = own[filled : filled + n_norms].reshape(n_norms * LANES)[:entries] / replicas
    velocity_norms = decay_rate * moment_norms + mean_norms
    updated_norms = weight_norms - step_rate * velocity_norms

    shard = lax.axis_index("shard")
    core = shard % 2
    query = own[n_table:filled].reshape(per_query, cols, LANES).transpose(1, 0, 2)
    query = jnp.pad(query, ((0, 0), (0, per_table - per_query), (0, 0))).reshape(n_table, LANES)
    both = jnp.stack([own[:n_table], query])
    both = jnp.broadcast_to(both[None], (shards // 2, 2, n_table, LANES)).reshape(shards, n_table, LANES)
    start = jnp.where(core == 0, start_table, start_query)
    gram = jnp.where(core == 0, gram_table, gram_query)
    total, start, gram, velocity_norms, updated_norms = lax.optimization_barrier(
        (exchange(both, "shard"), start, gram, velocity_norms, updated_norms)
    )
    total = total.reshape(shards, cols, per_table, LANES).transpose(0, 2, 1, 3)
    total = total.reshape(shards * per_table, width)

    stack = rank // ROWS
    used = cols * stack

    def reduce_right(basis):
        blocks = dot(basis, total, ((0,), (0,))).reshape(stack, ROWS, cols, LANES)
        blocks = blocks.transpose(2, 0, 1, 3).reshape(used, ROWS, LANES)
        blocks = jnp.pad(blocks, ((0, replicas - used), (0, 0), (0, 0)))
        return jnp.sum(exchange(blocks, "replica"), axis=0) / replicas

    basis = dot(dot(total, start, ((1,), (0,))) / replicas, gram[0], ((1,), (0,)))
    right = spread(reduce_right(basis), "replica")[:used]
    right = right.reshape(cols, stack, ROWS, LANES).transpose(1, 2, 0, 3).reshape(rank, width)
    basis = dot(dot(total, right, ((1,), (1,))) / replicas, gram[1], ((1,), (0,)))

    chip = lax.dynamic_slice_in_dim(basis, shard // 2 * (2 * per_table), 2 * per_table, 0)
    chip = jnp.concatenate([chip[i * ROWS : (i + 1) * ROWS] for i in range(2 * per_table // ROWS)], axis=1)
    mine = spread(jnp.concatenate([chip, reduce_right(basis)], axis=0), "replica")
    other = lax.ppermute(mine, "shard", [(i, i ^ 1) for i in range(shards)])
    (
        residual_table,
        velocity_table,
        updated_table,
        warm_table,
        residual_query,
        velocity_query,
        updated_query,
        warm_query,
    ) = finish(
        rank,
        8,
        core.reshape(1),
        mine,
        other,
        gradient_table[0],
        error_table[0],
        moment_table,
        weight_table,
        gradient_query[0],
        error_query[0],
        moment_query,
        weight_query,
    )
    return (
        residual_table[None],
        velocity_table,
        updated_table,
        warm_table.T,
        residual_query[None],
        velocity_query,
        updated_query,
        warm_query.T,
        velocity_norms,
        updated_norms,
    )


def solution(mesh):
    per_replica = P("replica", "shard", None)
    per_shard = P("shard", None)
    matrix = (per_replica, per_replica, per_shard, per_shard, P(), P())
    return jax.shard_map(
        local,
        mesh=mesh,
        in_specs=matrix + matrix + (P("replica", "shard"), P("shard"), P("shard")),
        out_specs=(per_replica, per_shard, per_shard, P()) * 2 + (P("shard"), P("shard")),
        check_vma=False,
    )
```

```python
import functools

import jax
import jax.numpy as jnp
from jax import lax
from jax.experimental import pallas as pl
from jax.experimental.pallas import tpu as pltpu
from jax.sharding import PartitionSpec as P

decay_rate = 0.9
step_rate = 0.01
LANES = 128
ROWS = 8
VMEM_LIMIT = 24 * 1024 * 1024
VMEM_ALL = 63 * 1024 * 1024


def dot(left, right, contract):
    return lax.dot_general(
        left,
        right,
        ((contract[0], contract[1]), ((), ())),
        precision=lax.Precision.HIGHEST,
        preferred_element_type=jnp.float32,
    )


def exchange(blocks, axis, groups=None):
    return lax.all_to_all(blocks, axis, 0, 0, axis_index_groups=groups)


def spread(block, axis):
    return exchange(jnp.broadcast_to(block[None], (lax.axis_size(axis),) + block.shape), axis)


def pack_kernel(first, gradient, error, rest, sent):
    total = gradient[...].astype(jnp.float32) + error[...]
    blocks = sent.shape[0]
    per = total.shape[0] // blocks
    cols = total.shape[1] // LANES
    for col in range(cols):
        piece = total[:, col * LANES : (col + 1) * LANES].reshape(blocks, per, LANES)
        sent[:, col * per : (col + 1) * per, :] = piece
    sent[:, cols * per :, :] = rest[...]


def pack(first, gradient, error, rest, steps):
    rows, width = gradient.shape
    blocks = rest.shape[0]
    height = rows // blocks * (width // LANES) + rest.shape[1]
    def source(i, first):
        return lax.rem(first[0] + i, steps)

    rows_spec = pl.BlockSpec((rows // steps, width), lambda i, first: (source(i, first), 0))
    return pl.pallas_call(
        pack_kernel,
        grid_spec=pltpu.PrefetchScalarGridSpec(
            num_scalar_prefetch=1,
            grid=(steps,),
            in_specs=[
                rows_spec,
                rows_spec,
                pl.BlockSpec((blocks // steps, rest.shape[1], LANES), lambda i, first: (source(i, first), 0, 0)),
            ],
            out_specs=pl.BlockSpec((blocks // steps, height, LANES), lambda i, first: (i, 0, 0)),
        ),
        out_shape=jax.ShapeDtypeStruct((blocks, height, LANES), jnp.float32),
        compiler_params=pltpu.CompilerParams(vmem_limit_bytes=VMEM_LIMIT),
        name="pack",
    )(first, gradient, error, rest)


def apply(approx, merged, moment, weight, residual, velocity, updated):
    residual[...] = merged - approx
    speed = decay_rate * moment + approx
    velocity[...] = speed
    updated[...] = weight - step_rate * speed


def finish_kernel(
    rank, core, mine, other, gt, et, vt, wt, gq, eq, vq, wq,
    rt_out, vt_out, ut_out, warm_table, rq_out, vq_out, uq_out, warm_query, tiles,
):
    step = pl.program_id(0)
    replicas = mine.shape[0]
    width = gt.shape[1]
    cols = width // LANES
    stack = rank // ROWS

    def pick(first, second):
        return jnp.where(core[0] == 0, first, second)

    def own(part):
        flat = part.reshape(replicas * ROWS, LANES)
        return pick(flat, pltpu.roll(flat, LANES // 2, 1)).reshape(replicas, ROWS, LANES)

    @pl.when(step == 0)
    def _():
        here, there = mine[...], other[...]
        for out, block in ((warm_table, pick(here, there)), (warm_query, pick(there, here))):
            for col in range(cols):
                for row in range(stack):
                    piece = block[col * stack + row, ROWS:, :]
                    out[row * ROWS : (row + 1) * ROWS, col * LANES : (col + 1) * LANES] = piece
        tiles[0] = own(pick(here[:, :ROWS, :], there[:, :ROWS, :]))
        tiles[1] = own(pick(there[:, :ROWS, :], here[:, :ROWS, :]))
        for i in range(gq.shape[0] // replicas):
            part = pl.ds(i * replicas, replicas)
            basis = tiles[1, :, i, :][:, :rank]
            merged = gq[part, :].astype(jnp.float32) + eq[part, :]
            apply(
                dot(basis, warm_query[...], ((1,), (0,))),
                merged,
                vq[part, :],
                wq[part, :],
                rq_out.at[part, :],
                vq_out.at[part, :],
                uq_out.at[part, :],
            )

    some = gt.shape[0] // (2 * ROWS)
    tile = tiles[0, pl.ds(pl.multiple_of(step * some, some), some)].reshape(some * ROWS, LANES)
    halves = [
        dot(tile[:, h * rank : (h + 1) * rank], warm_table[...], ((1,), (0,))).reshape(some, 1, ROWS, width)
        for h in range(2)
    ]
    approx = jnp.concatenate(halves, axis=1).reshape(2 * some * ROWS, width)
    merged = gt[...].astype(jnp.float32) + et[...]
    apply(approx, merged, vt[...], wt[...], rt_out, vt_out, ut_out)


def finish(rank, steps, core, mine, other, gt, et, vt, wt, gq, eq, vq, wq):
    rows, width = gt.shape
    rows_query = gq.shape[0]
    moving = pl.BlockSpec((rows // steps, width), lambda i: (i, 0))
    fixed = pl.BlockSpec((rows_query, width), lambda i: (0, 0))
    factor = pl.BlockSpec((rank, width), lambda i: (0, 0))
    whole = pl.BlockSpec(mine.shape, lambda i: (0, 0, 0))
    shape = functools.partial(jax.ShapeDtypeStruct, dtype=jnp.float32)
    return pl.pallas_call(
        functools.partial(finish_kernel, rank),
        grid=(steps,),
        in_specs=[pl.BlockSpec(memory_space=pltpu.SMEM), whole, whole] + [moving] * 4 + [fixed] * 4,
        out_specs=[moving] * 3 + [factor] + [fixed] * 3 + [factor],
        out_shape=[shape((rows, width))] * 3
        + [shape((rank, width))]
        + [shape((rows_query, width))] * 3
        + [shape((rank, width))],
        scratch_shapes=[pltpu.VMEM((2, mine.shape[0], ROWS, LANES), jnp.float32)],
        compiler_params=pltpu.CompilerParams(vmem_limit_bytes=VMEM_ALL),
        name="finish",
    )(core, mine, other, gt, et, vt, wt, gq, eq, vq, wq)


def local(
    gradient_table,
    error_table,
    moment_table,
    weight_table,
    start_table,
    gram_table,
    gradient_query,
    error_query,
    moment_query,
    weight_query,
    start_query,
    gram_query,
    gradient_norms,
    moment_norms,
    weight_norms,
):
    replicas = lax.axis_size("replica")
    shards = lax.axis_size("shard")
    rows_table, width = moment_table.shape
    rows_query = moment_query.shape[0]
    rank = start_table.shape[1]
    cols = width // LANES
    per_table = rows_table // replicas
    per_query = rows_query // replicas
    entries = moment_norms.shape[0]
    fours, eights = 4, replicas // 4
    along = [[eights * first + second for second in range(eights)] for first in range(fours)]

    n_table = per_table * cols
    n_query = per_query * cols
    n_norms = -(-entries // LANES)
    filled = n_table + n_query
    height = -(-(filled + n_norms) // ROWS) * ROWS
    merged_query = gradient_query[0].astype(jnp.float32) + error_query[0]
    rest = merged_query.reshape(per_query, replicas, cols, LANES).transpose(1, 0, 2, 3)
    norms = jnp.pad(gradient_norms, ((0, 0), (0, n_norms * LANES - entries))).reshape(1, n_norms, LANES)
    norms = jnp.broadcast_to(norms, (replicas, n_norms, LANES))
    rest = jnp.concatenate([rest.reshape(replicas, n_query, LANES), norms], axis=1)
    rest = jnp.pad(rest, ((0, 0), (0, height - filled - n_norms), (0, 0)))
    first = lax.axis_index("replica") // eights
    sent = pack(first.reshape(1), gradient_table[0], error_table[0], rest, fours)
    sent = sent.reshape(fours, 2, eights // 2, height, LANES)

    def shift(block, by):
        pairs = [(f * eights + e, (f + by) % fours * eights + e) for f in range(fours) for e in range(eights)]
        return lax.ppermute(block, "replica", pairs)

    ahead = shift(sent[2, 0], 1)
    back = shift(sent[2, 1], fours - 1)
    right_one = shift(sent[1, 1], 1)
    left_zero = shift(sent[3, 0], fours - 1)
    right_zero = shift(sent[1, 0] + ahead, 1)
    left_one = shift(sent[3, 1] + back, fours - 1)
    zero = sent[0, 0] + left_zero + right_zero
    one = sent[0, 1] + right_one + left_one
    blocks = jnp.concatenate([zero, one], axis=0)
    own = jnp.sum(exchange(blocks, "replica", along), axis=0)

    mean_norms = own[filled : filled + n_norms].reshape(n_norms * LANES)[:entries] / replicas
    velocity_norms = decay_rate * moment_norms + mean_norms
    updated_norms = weight_norms - step_rate * velocity_norms

    shard = lax.axis_index("shard")
    core = shard % 2
    query = own[n_table:filled].reshape(per_query, cols, LANES).transpose(1, 0, 2)
    query = jnp.pad(query, ((0, 0), (0, per_table - per_query), (0, 0))).reshape(n_table, LANES)
    both = jnp.stack([own[:n_table], query])
    both = jnp.broadcast_to(both[None], (shards // 2, 2, n_table, LANES)).reshape(shards, n_table, LANES)
    start = jnp.where(core == 0, start_table, start_query)
    gram = jnp.where(core == 0, gram_table, gram_query)
    total, start, gram, velocity_norms, updated_norms = lax.optimization_barrier(
        (exchange(both, "shard"), start, gram, velocity_norms, updated_norms)
    )
    total = total.reshape(shards, cols, per_table, LANES).transpose(0, 2, 1, 3)
    total = total.reshape(shards * per_table, width)

    stack = rank // ROWS
    used = cols * stack

    def reduce_right(basis):
        blocks = dot(basis, total, ((0,), (0,))).reshape(stack, ROWS, cols, LANES)
        blocks = blocks.transpose(2, 0, 1, 3).reshape(used, ROWS, LANES)
        blocks = jnp.pad(blocks, ((0, replicas - used), (0, 0), (0, 0)))
        return jnp.sum(exchange(blocks, "replica"), axis=0) / replicas

    basis = dot(dot(total, start, ((1,), (0,))) / replicas, gram[0], ((1,), (0,)))
    right = spread(reduce_right(basis), "replica")[:used]
    right = right.reshape(cols, stack, ROWS, LANES).transpose(1, 2, 0, 3).reshape(rank, width)
    basis = dot(dot(total, right, ((1,), (1,))) / replicas, gram[1], ((1,), (0,)))

    chip = lax.dynamic_slice_in_dim(basis, shard // 2 * (2 * per_table), 2 * per_table, 0)
    chip = jnp.concatenate([chip[i * ROWS : (i + 1) * ROWS] for i in range(2 * per_table // ROWS)], axis=1)
    mine = spread(jnp.concatenate([chip, reduce_right(basis)], axis=0), "replica")
    other = lax.ppermute(mine, "shard", [(i, i ^ 1) for i in range(shards)])
    (
        residual_table,
        velocity_table,
        updated_table,
        warm_table,
        residual_query,
        velocity_query,
        updated_query,
        warm_query,
    ) = finish(
        rank,
        4,
        core.reshape(1),
        mine,
        other,
        gradient_table[0],
        error_table[0],
        moment_table,
        weight_table,
        gradient_query[0],
        error_query[0],
        moment_query,
        weight_query,
    )
    return (
        residual_table[None],
        velocity_table,
        updated_table,
        warm_table.T,
        residual_query[None],
        velocity_query,
        updated_query,
        warm_query.T,
        velocity_norms,
        updated_norms,
    )


def solution(mesh):
    per_replica = P("replica", "shard", None)
    per_shard = P("shard", None)
    matrix = (per_replica, per_replica, per_shard, per_shard, P(), P())
    return jax.shard_map(
        local,
        mesh=mesh,
        in_specs=matrix + matrix + (P("replica", "shard"), P("shard"), P("shard")),
        out_specs=(per_replica, per_shard, per_shard, P()) * 2 + (P("shard"), P("shard")),
        check_vma=False,
    )
```
